128 devices in a mesh: blk: 32 (over x, z, core), tok: 4 (over y).
Axes of the slice: x: 4, y: 4, z: 4, core: 2. Of those that a mesh axis runs over, the one named last changes fastest.
Arguments:
- stream: bfloat16 [16384, 1664], P(('tok', 'blk'))
- queries: bfloat16 [16384, 1664], P(('tok', 'blk'))
- key_cache: bfloat16 [16384, 1664], P(('tok', 'blk'))
- value_cache: bfloat16 [16384, 1664], P(('tok', 'blk')), may hold values from -6 to 6
- segments: int32 [16384], P('tok'), may hold values from 63 to 16383, as said below
- stale_rows: int32 [1536], P(('tok', 'blk')), may hold values from 0 to 16383, as said below
- owners: int32 [4096], P(('tok', 'blk')), may hold values from 0 to 3, as said below
- attn_gain: float32 [1664], replicated, may hold values from 0.1 to 1.9
- w_key: bfloat16 [1664, 1664], replicated, may hold values from -0.15625 to 0.15625
- key_bias: float32 [1664], replicated, may hold values from -3 to 3
- mlp_gain: float32 [1664], replicated, may hold values from 0.1 to 1.9
- w_fc: bfloat16 [1664, 8192], P(None, 'blk'), may hold values from -0.15625 to 0.15625
- b_fc: float32 [8192], P('blk'), may hold values from -3 to 3
- w_proj: bfloat16 [8192, 1664], P('blk'), may hold values from -0.125 to 0.125
- b_proj: float32 [1664], replicated, may hold values from -3 to 3
- merge_gain: float32 [1664], replicated, may hold values from 0.1 to 1.9
- w_merge: bfloat16 [1664, 1664], replicated, may hold values from -0.15625 to 0.15625
- b_merge: float32 [1664], replicated, may hold values from -3 to 3
Outputs:
- refreshed_keys: bfloat16 [16384, 1664], P(('tok', 'blk'))
- delivered: bfloat16 [4, 32, 128, 1664], P('tok', 'blk')
The draws below stay inside these ranges and needn't reach their ends.
Inputs may be any that keep to these rules, and one draw needn't show every extreme that they name: `segments`: A segment's id is the index of its last row, so ids never fall; each segment has 4 to 128 rows, a multiple of 4, and lies inside one aligned block of 4096 rows; each such block begins with a segment of 64 rows followed by one of exactly 128 rows. `stale_rows`: Distinct; the aligned block of 128 rows of each device holds exactly 12 of them, all inside that block and listed on that device; row 0 and the last row are always listed. `owners`: all merged tokens of one segment (the segment of row 4 m for merged token m) have the same owner.
All inputs are finite; a program needn't handle non-finite values.
Results may differ from the reference program's by a relative error of at most 0.011.
Values may be sent and summed in bfloat16 or wider, within the bound.
No kernel may reach another device: no remote copies, remote signals or barrier semaphores. Data moves between devices by JAX's collectives and lax.ppermute only.
A program may use at most 192 MiB of HBM per device.

```python
import math
import jax
import jax.numpy as jnp
from jax import lax

D = 1664
HEADS = 16
HEAD_DIM = 104
FF = 8192
TOK_DEV = 128
TOKENS = 16384
MERGED_DEV = 32
REF_DEV = 12
N_BLK = 32
N_TOK = 4


def segment_ids(key):
    group_rows = TOKENS // N_TOK
    most_segs = group_rows // 4
    lengths = 4 * jax.random.randint(key, (N_TOK, most_segs), 1, TOK_DEV // 4 + 1)
    lengths = lengths.at[:, 0].set(TOK_DEV // 2)
    lengths = lengths.at[:, 1].set(TOK_DEV)
    bounds = jnp.cumsum(lengths, axis=1)
    places = jnp.arange(group_rows, dtype=jnp.int32)
    local_ids = jnp.sum((bounds[:, None, :] <= places[None, :, None]).astype(jnp.int32), axis=2)
    ends = jnp.minimum(jnp.take_along_axis(bounds, local_ids, axis=1), group_rows) - 1
    offsets = jnp.arange(N_TOK, dtype=jnp.int32)[:, None] * group_rows
    return (ends + offsets).reshape(TOKENS).astype(jnp.int32)


def draw_segments(key, part):
    return segment_ids(jax.random.fold_in(key, 11))


def draw_owners(key, part):
    seg_ids = segment_ids(jax.random.fold_in(key, 11))
    picks = jax.random.randint(jax.random.fold_in(key, 12), (TOKENS,), 0, 2 * N_TOK - 1)
    levels = jnp.maximum(picks - N_TOK + 1, 0)
    turned = jax.random.randint(jax.random.fold_in(key, 13), (), 0, N_TOK)
    table = (levels + turned) % N_TOK
    return table[seg_ids[::4]].astype(jnp.int32)


def draw_stale_rows(key, part):
    blocks = TOKENS // TOK_DEV
    block_keys = jax.random.split(jax.random.fold_in(key, 14), blocks)
    block_ids = jnp.arange(blocks, dtype=jnp.int32)
    targets = jnp.where(block_ids == 0, 0, jnp.where(block_ids == blocks - 1, TOK_DEV - 1, -1)).astype(jnp.int32)

    def one_block(single, target):
        order = jax.random.permutation(single, TOK_DEV).astype(jnp.int32)
        found = jnp.argmax(order == target).astype(jnp.int32)
        turn = jnp.where(target >= 0, found, 0)
        return jnp.roll(order, -turn)[:REF_DEV]
    picks = jax.vmap(one_block)(block_keys, targets)
    return (picks + block_ids[:, None] * TOK_DEV).reshape(-1).astype(jnp.int32)


def paired_fields(key):
    key_first = jax.random.fold_in(key, 21)
    key_second = jax.random.fold_in(key, 22)
    key_out = jnp.clip(jax.random.normal(key_first, (TOKENS, D), jnp.float32), -6.0, 6.0)
    query_out = jnp.clip(jax.random.normal(key_second, (TOKENS, D), jnp.float32), -6.0, 6.0)
    return (query_out, key_out)


def draw_queries(key, part):
    return paired_fields(key)[0].astype(jnp.bfloat16)


def draw_key_cache(key, part):
    return paired_fields(key)[1].astype(jnp.bfloat16)


def draw_stream(key, part):
    row_scale = jnp.exp(jax.random.uniform(jax.random.fold_in(key, 31), (TOKENS, 1), jnp.float32, 0.0, math.log(10.0)))
    col_scale = jnp.exp(jax.random.uniform(jax.random.fold_in(key, 32), (1, D), jnp.float32, 0.0, math.log(10.0)))
    base = jnp.clip(jax.random.normal(jax.random.fold_in(key, 33), (TOKENS, D), jnp.float32), -6.0, 6.0)
    return (0.3 * base * row_scale * col_scale).astype(jnp.bfloat16)


def block_levels(own_key, shape, cuts, least, largest):
    level = 1.0
    for position, blocks in cuts:
        heights = jax.random.uniform(jax.random.fold_in(jax.random.fold_in(own_key, 6), position), (blocks,), jnp.float32, least / len(cuts), largest / len(cuts))
        level = level * jnp.repeat(jnp.exp(heights), shape[position] // blocks).reshape((-1,) + (1,) * (len(shape) - 1 - position))
    return level


def bell_draw(rng, shape, width, most, cuts=(), kind=jnp.bfloat16):
    result = jax.random.normal(rng, shape, jnp.float32) * width
    if len(cuts) > 0:
        result = block_levels(rng, shape, cuts, -0.22, 0.18) * result
    return jnp.clip(result, min=-most, max=most).astype(kind)


def setup_inputs(seed: int = 0) -> dict:
    key_of = jax.random.split(jax.random.key(seed), 19)
    stream = draw_stream(jax.random.fold_in(key_of[18], 71), 0)
    queries = draw_queries(jax.random.fold_in(key_of[18], 71), 0)
    key_cache = draw_key_cache(jax.random.fold_in(key_of[18], 71), 0)
    value_cache = bell_draw(key_of[3], (TOKENS, D), 1.0, 6.0, ((0, 128),))
    segments = draw_segments(jax.random.fold_in(key_of[18], 71), 0)
    stale_rows = draw_stale_rows(jax.random.fold_in(key_of[18], 71), 0)
    owners = draw_owners(jax.random.fold_in(key_of[18], 71), 0)
    attn_gain = jnp.clip(1.0 + 0.18 * jax.random.normal(key_of[7], (D,), jnp.float32), 0.1, 1.9)
    w_key = bell_draw(key_of[8], (D, D), D ** -0.5, 0.15625)
    key_bias = bell_draw(key_of[9], (D,), 0.5, 3.0, (), jnp.float32)
    mlp_gain = jnp.clip(1.0 + 0.18 * jax.random.normal(key_of[10], (D,), jnp.float32), 0.1, 1.9)
    w_fc = bell_draw(key_of[11], (D, FF), D ** -0.5, 0.15625, ((1, 32),))
    b_fc = bell_draw(key_of[12], (FF,), 0.5, 3.0, ((0, 32),), jnp.float32)
    w_proj = bell_draw(key_of[13], (FF, D), (FF // 4) ** -0.5, 0.125, ((0, 32),))
    b_proj = bell_draw(key_of[14], (D,), 0.5, 3.0, (), jnp.float32)
    merge_gain = jnp.clip(1.0 + 0.18 * jax.random.normal(key_of[15], (D,), jnp.float32), 0.1, 1.9)
    w_merge = bell_draw(key_of[16], (D, D), D ** -0.5, 0.15625)
    b_merge = bell_draw(key_of[17], (D,), 0.5, 3.0, (), jnp.float32)
    return {"stream": stream, "queries": queries, "key_cache": key_cache, "value_cache": value_cache, "segments": segments, "stale_rows": stale_rows, "owners": owners, "attn_gain": attn_gain, "w_key": w_key, "key_bias": key_bias, "mlp_gain": mlp_gain, "w_fc": w_fc, "b_fc": b_fc, "w_proj": w_proj, "b_proj": b_proj, "merge_gain": merge_gain, "w_merge": w_merge, "b_merge": b_merge}


def layer_norm(values, gain):
    center = values - lax.optimization_barrier(jnp.mean(values, axis=-1, keepdims=True))
    spread = lax.optimization_barrier(jnp.mean(center * center, axis=-1, keepdims=True))
    return center * lax.rsqrt(spread + 1e-06) * gain

def reference(stream, queries, key_cache, value_cache, segments, stale_rows, owners, attn_gain, w_key, key_bias, mlp_gain, w_fc, b_fc, w_proj, b_proj, merge_gain, w_merge, b_merge):
    held = layer_norm(stream[stale_rows].astype(jnp.float32), attn_gain).astype(jnp.bfloat16)
    fresh_keys = (jnp.dot(held, w_key, preferred_element_type=jnp.float32) + key_bias).astype(jnp.bfloat16)
    refreshed = key_cache.at[stale_rows].set(fresh_keys)
    blocks = TOKENS // TOK_DEV
    zero_rows = jnp.zeros((TOK_DEV, D), jnp.bfloat16)
    key_padded = jnp.concatenate([zero_rows, refreshed, zero_rows], axis=0)
    value_padded = jnp.concatenate([zero_rows, value_cache, zero_rows], axis=0)
    minus_ones = jnp.full((TOK_DEV,), -1, jnp.int32)
    seg_padded = jnp.concatenate([minus_ones, segments.astype(jnp.int32), minus_ones], axis=0)
    factor = 1.0 / HEAD_DIM ** 0.5

    def one_block(index):
        first = (index * TOK_DEV).astype(jnp.int32)
        query_block = lax.dynamic_slice_in_dim(queries, first, TOK_DEV, 0).reshape(TOK_DEV, HEADS, HEAD_DIM).astype(jnp.float32)
        key_block = lax.dynamic_slice_in_dim(key_padded, first, 3 * TOK_DEV, 0).reshape(3 * TOK_DEV, HEADS, HEAD_DIM).astype(jnp.float32)
        value_block = lax.dynamic_slice_in_dim(value_padded, first, 3 * TOK_DEV, 0).reshape(3 * TOK_DEV, HEADS, HEAD_DIM).astype(jnp.float32)
        query_seg = lax.dynamic_slice_in_dim(segments.astype(jnp.int32), first, TOK_DEV, 0)
        key_seg = lax.dynamic_slice_in_dim(seg_padded, first, 3 * TOK_DEV, 0)
        scores = jnp.einsum('qhd,khd->hqk', query_block, key_block) * factor
        allowed = (query_seg[:, None] == key_seg[None, :])[None]
        scores = jnp.where(allowed, scores, -jnp.inf)
        top = lax.optimization_barrier(jnp.max(scores, axis=-1, keepdims=True))
        weights = jnp.exp(scores - top)
        probs = (weights / lax.optimization_barrier(jnp.sum(weights, axis=-1, keepdims=True))).astype(jnp.bfloat16)
        output = jnp.einsum('hqk,khd->qhd', probs.astype(jnp.float32), value_block)
        return output.reshape(TOK_DEV, D).astype(jnp.bfloat16)
    attended = lax.map(one_block, jnp.arange(blocks, dtype=jnp.int32)).reshape(TOKENS, D)
    mixed = stream.astype(jnp.float32) + attended.astype(jnp.float32)
    normed = layer_norm(mixed, mlp_gain).astype(jnp.bfloat16)
    units = jax.nn.gelu(jnp.dot(normed, w_fc, preferred_element_type=jnp.float32) + b_fc, approximate=False).astype(jnp.bfloat16)
    summed = jnp.dot(units, w_proj, preferred_element_type=jnp.float32)
    pooled = lax.optimization_barrier(jnp.mean((mixed + summed).reshape(TOKENS // 4, 4, D), axis=1)) + b_proj
    merge_in = layer_norm(pooled, merge_gain).astype(jnp.bfloat16)
    merged = (jnp.dot(merge_in, w_merge, preferred_element_type=jnp.float32) + b_merge).astype(jnp.bfloat16)
    merged_grid = merged.reshape(N_TOK, N_BLK, MERGED_DEV, D).astype(jnp.float32)
    owner_grid = owners.astype(jnp.int32).reshape(N_TOK, N_BLK, MERGED_DEV)
    owner_hot = (owner_grid[..., None] == jnp.arange(N_TOK, dtype=jnp.int32)).astype(jnp.int32)
    ranking = lax.optimization_barrier(jnp.sum(jnp.cumsum(owner_hot, axis=2) * owner_hot, axis=-1)) - 1
    picked = (owner_grid[:, :, None, None, :] == jnp.arange(N_TOK, dtype=jnp.int32)[None, None, :, None, None]) & (ranking[:, :, None, None, :] == jnp.arange(MERGED_DEV, dtype=jnp.int32)[None, None, None, :, None])
    placed = jnp.einsum('tbosm,tbmd->obtsd', picked.astype(jnp.float32), merged_grid)
    delivered = placed.astype(jnp.bfloat16).reshape(N_TOK, N_BLK, N_TOK * MERGED_DEV, D)
    return (refreshed, delivered)
```

```python
import jax
import jax.numpy as jnp
from jax import lax
from jax.sharding import Mesh
from jax.sharding import PartitionSpec as P

HEADS = 16
ROWS = ("tok", "x", "z", "c")


def passed_along(block, axes, distance):
    count = 1
    for axis in axes:
        count *= lax.axis_size(axis)
    route = [(i - distance, i) for i in range(count) if 0 <= i - distance < count]
    return lax.ppermute(block, axes, route)


def layer_norm(values, gain):
    center = values - jnp.mean(values, axis=-1, keepdims=True)
    spread = jnp.mean(center * center, axis=-1, keepdims=True)
    return center * lax.rsqrt(spread + 1e-06) * gain


def body(
    stream,
    queries,
    key_cache,
    value_cache,
    segments,
    stale_rows,
    owners,
    attn_gain,
    w_key,
    key_bias,
    mlp_gain,
    w_fc,
    b_fc,
    w_proj,
    b_proj,
    merge_gain,
    w_merge,
    b_merge,
):
    row_count = stream.shape[0]
    model_width = stream.shape[1]
    head_size = model_width // HEADS
    tok_count = lax.axis_size("tok")
    x_count = lax.axis_size("x")
    tok = lax.axis_index("tok")
    units_here = w_fc.shape[1]

    fc_part = model_width // tok_count
    fc_piece = lax.dynamic_slice_in_dim(w_fc, tok * fc_part, fc_part, 0)
    fc_all = lax.all_gather(fc_piece, ("x", "tok"), axis=0, tiled=True)
    fc_all = fc_all.reshape(x_count, model_width, units_here)
    proj_part = units_here // tok_count
    proj_piece = lax.dynamic_slice_in_dim(w_proj, tok * proj_part, proj_part, 0)
    proj_all = lax.all_gather(proj_piece, ("x", "tok"), axis=0, tiled=True)
    bias_all = lax.all_gather(b_fc, "x", axis=0, tiled=True)

    local_rows = stale_rows % row_count
    held = layer_norm(stream[local_rows].astype(jnp.float32), attn_gain).astype(jnp.bfloat16)
    fresh_keys = (jnp.dot(held, w_key, preferred_element_type=jnp.float32) + key_bias).astype(
        jnp.bfloat16
    )
    refreshed = key_cache.at[local_rows].set(fresh_keys)
    blk = ("x", "z", "c")
    below = passed_along((refreshed, value_cache), blk, 1)
    above = passed_along((refreshed, value_cache), blk, -1)
    key_window = jnp.concatenate([below[0], refreshed, above[0]], axis=0).reshape(
        3 * row_count, HEADS, head_size
    )
    value_window = jnp.concatenate([below[1], value_cache, above[1]], axis=0).reshape(
        3 * row_count, HEADS, head_size
    )
    position = lax.axis_index(blk)
    minus_ones = jnp.full((row_count,), -1, jnp.int32)
    seg_padded = jnp.concatenate([minus_ones, segments, minus_ones], axis=0)
    key_seg = lax.dynamic_slice_in_dim(seg_padded, position * row_count, 3 * row_count, 0)
    query_seg = lax.dynamic_slice_in_dim(segments, position * row_count, row_count, 0)
    query_heads = queries.reshape(row_count, HEADS, head_size)
    scores = jnp.einsum(
        "qhd,khd->hqk", query_heads, key_window, preferred_element_type=jnp.float32
    ) * (1.0 / head_size**0.5)
    allowed = (query_seg[:, None] == key_seg[None, :])[None]
    scores = jnp.where(allowed, scores, -jnp.inf)
    top_score = jnp.max(scores, axis=-1, keepdims=True)
    weights = jnp.exp(scores - top_score)
    probs = (weights / jnp.sum(weights, axis=-1, keepdims=True)).astype(jnp.bfloat16)
    attended = jnp.einsum("hqk,khd->qhd", probs, value_window, preferred_element_type=jnp.float32)
    attended = attended.reshape(row_count, model_width).astype(jnp.bfloat16)
    mixed = stream.astype(jnp.float32) + attended.astype(jnp.float32)
    normed = layer_norm(mixed, mlp_gain).astype(jnp.bfloat16)

    rows = lax.all_gather(normed, ("z", "c"), axis=0, tiled=True)
    group_rows = rows.shape[0]
    pooled_units = []
    for i in range(x_count):
        bias = lax.slice_in_dim(bias_all, i * units_here, (i + 1) * units_here)
        units = jax.nn.gelu(
            jnp.dot(rows, fc_all[i], preferred_element_type=jnp.float32) + bias,
            approximate=False,
        ).astype(jnp.bfloat16)
        pooled_units.append(
            jnp.mean(units.astype(jnp.float32).reshape(group_rows // 4, 4, units_here), axis=1)
        )
    pooled_units = jnp.concatenate(pooled_units, axis=1).astype(jnp.bfloat16)
    partial = jnp.dot(pooled_units, proj_all, preferred_element_type=jnp.float32)
    summed = lax.psum_scatter(
        partial.astype(jnp.bfloat16), ("z", "c"), scatter_dimension=0, tiled=True
    ).astype(jnp.float32)
    pooled = jnp.mean(mixed.reshape(row_count // 4, 4, model_width), axis=1) + summed + b_proj
    merge_in = layer_norm(pooled, merge_gain).astype(jnp.bfloat16)
    merged = (jnp.dot(merge_in, w_merge, preferred_element_type=jnp.float32) + b_merge).astype(
        jnp.bfloat16
    )
    merged_rows = row_count // 4
    owner_hot = (owners[:, None] == jnp.arange(tok_count, dtype=jnp.int32)[None, :]).astype(
        jnp.int32
    )
    ranking = jnp.sum(jnp.cumsum(owner_hot, axis=0) * owner_hot, axis=-1) - 1
    selector = (
        owners[None, None, :] == jnp.arange(tok_count, dtype=jnp.int32)[:, None, None]
    ) & (ranking[None, None, :] == jnp.arange(merged_rows, dtype=jnp.int32)[None, :, None])
    outgoing = jnp.einsum(
        "osm,md->osd", selector.astype(jnp.bfloat16), merged, preferred_element_type=jnp.float32
    ).astype(jnp.bfloat16)
    arrived = lax.all_to_all(outgoing, "tok", split_axis=0, concat_axis=0, tiled=True)
    delivered = arrived.reshape(1, 1, tok_count * merged_rows, model_width)
    return (refreshed, delivered)


def solution(mesh):
    fine = Mesh(mesh.devices.reshape(4, 4, 2, 4), ("x", "z", "c", "tok"))
    blk = ("x", "z", "c")
    return jax.shard_map(
        body,
        mesh=fine,
        in_specs=(
            P(ROWS, None),
            P(ROWS, None),
            P(ROWS, None),
            P(ROWS, None),
            P("tok"),
            P(ROWS),
            P(ROWS),
            P(),
            P(),
            P(),
            P(),
            P(None, blk),
            P(blk),
            P(blk, None),
            P(),
            P(),
            P(),
            P(),
        ),
        out_specs=(P(ROWS, None), P("tok", blk, None, None)),
        check_vma=False,
    )
```

```python
import jax
import jax.numpy as jnp
from jax import lax
from jax.experimental import pallas as pl
from jax.experimental.pallas import tpu as pltpu
from jax.sharding import Mesh
from jax.sharding import PartitionSpec as P

HEADS = 16
ROWS = ("tok", "x", "z", "c")
BLK = ("x", "z", "c")
FC_CUT = 768


def passed_along(block, distance):
    count = lax.axis_size("x") * lax.axis_size("z") * lax.axis_size("c")
    route = [(i - distance, i) for i in range(count) if 0 <= i - distance < count]
    return lax.ppermute(block, BLK, route)


def shift(block, axis, distance):
    count = lax.axis_size(axis)
    return lax.ppermute(block, axis, [(i, (i + distance) % count) for i in range(count)])


def layer_norm(values, gain):
    center = values - jnp.mean(values, axis=-1, keepdims=True)
    spread = jnp.mean(center * center, axis=-1, keepdims=True)
    return center * lax.rsqrt(spread + 1e-06) * gain


def three_terms(values):
    high = values.astype(jnp.bfloat16)
    rest = values - high.astype(jnp.float32)
    middle = rest.astype(jnp.bfloat16)
    low = (rest - middle.astype(jnp.float32)).astype(jnp.bfloat16)
    return jnp.stack([high, middle, low])


def dot(left, right):
    return jnp.dot(left, right, preferred_element_type=jnp.float32)


def iota(shape, axis):
    return lax.broadcasted_iota(jnp.int32, shape, axis)


def mean_of_fours(rows):
    hit = iota((rows // 4, rows), 1) // 4 == iota((rows // 4, rows), 0)
    return jnp.where(hit, 0.25, 0.0).astype(jnp.bfloat16)


def call(kernel, outs, name, flops, limit, *args):
    moved = sum(a.size * a.dtype.itemsize for a in args)
    return pl.pallas_call(
        kernel,
        out_shape=outs,
        in_specs=[pl.BlockSpec(memory_space=pltpu.VMEM) for _ in args],
        out_specs=jax.tree.map(lambda _: pl.BlockSpec(memory_space=pltpu.VMEM), outs),
        compiler_params=pltpu.CompilerParams(vmem_limit_bytes=limit << 20),
        cost_estimate=pl.CostEstimate(flops=flops, bytes_accessed=moved, transcendentals=0),
        name=name,
    )(*args)


def refresh_kernel(stream, keys, rows_col, rows_row, gain, w_key, key_bias, out):
    count = rows_col.shape[0]
    block = stream.shape[0]
    pick = jnp.where(rows_col[...] == iota((count, block), 1), 1.0, 0.0).astype(jnp.bfloat16)
    held = layer_norm(dot(pick, stream[...]), gain[...]).astype(jnp.bfloat16)
    fresh = (dot(held, w_key[...]) + key_bias[...]).astype(jnp.bfloat16)
    place = jnp.where(rows_row[...] == iota((block, count), 0), 1.0, 0.0)
    hit = jnp.sum(place, axis=1, keepdims=True) > 0.5
    spread = dot(place.astype(jnp.bfloat16), fresh)
    old = keys[...].astype(jnp.float32)
    out[...] = jnp.where(hit, spread, old).astype(jnp.bfloat16)


def attention_kernel(
    queries,
    keys_below,
    keys,
    keys_above,
    values_below,
    values,
    values_above,
    stream,
    seg_col,
    seg_row,
    gain,
    normed,
    mixed_mean,
    attended,
):
    rows, width = queries.shape
    size = width // HEADS
    allowed = seg_col[...] == seg_row[...]
    scale = 1.0 / size**0.5
    for h in range(HEADS):
        low = h * size // 128 * 128
        high = min(-(-(h + 1) * size // 128) * 128, width)
        lane = iota((1, high - low), 1) + low
        mine = (lane >= h * size) & (lane < (h + 1) * size)
        picked = jnp.where(mine, 1.0, 0.0).astype(jnp.bfloat16)
        query = queries[:, low:high] * picked
        key = jnp.concatenate(
            [keys_below[:, low:high], keys[:, low:high], keys_above[:, low:high]], axis=0
        )
        value = jnp.concatenate(
            [values_below[:, low:high], values[:, low:high], values_above[:, low:high]], axis=0
        )
        scores = lax.dot_general(
            query, key, (((1,), (1,)), ((), ())), preferred_element_type=jnp.float32
        )
        scores = jnp.where(allowed, scores * scale, -jnp.inf)
        weights = jnp.exp(scores - jnp.max(scores, axis=-1, keepdims=True))
        share = 1.0 / jnp.sum(weights, axis=-1, keepdims=True)
        found = dot((weights * share).astype(jnp.bfloat16), value)
        attended[:, low:high] = jnp.where(mine, found, attended[:, low:high])
    rounded = attended[...].astype(jnp.bfloat16)
    fours = mean_of_fours(rows)
    mixed_mean[...] = dot(fours, stream[...]) + dot(fours, rounded)
    mixed = stream[...].astype(jnp.float32) + rounded.astype(jnp.float32)
    normed[...] = layer_norm(mixed, gain[...]).astype(jnp.bfloat16)


def mlp_kernel(counts, here, *refs):
    row_refs = refs[: sum(counts)]
    own, left, right, far_a, far_b, proj = refs[sum(counts) : sum(counts) + 6]
    outs = refs[sum(counts) + 6 :]
    width = row_refs[0].shape[1]
    shards, depth, _ = proj.shape
    x = here[0]
    sides = []
    at = 0
    for count, out in zip(counts, outs):
        group = row_refs[at : at + count]
        at += count
        chunk, chunk_rows = [], 0
        done = 0
        for ref in group:
            chunk.append(ref)
            chunk_rows += ref.shape[0]
            if chunk_rows == 256 or ref is group[-1]:
                sides.append((tuple(chunk), chunk_rows, out, done))
                done += chunk_rows // 4
                chunk, chunk_rows = [], 0
    if len(sides) == 2 and sides[0][1] + sides[1][1] <= 256:
        passes = [sides]
    else:
        passes = [[side] for side in sides]
    for parts in passes:
        rows = jnp.concatenate([ref[...] for part in parts for ref in part[0]], axis=0)
        fours = mean_of_fours(rows.shape[0])
        total = None
        for number, (fc, step) in enumerate(
            ((own, 0), (left, shards - 1), (right, 1), (None, 2))
        ):
            if fc is not None:
                terms = fc[width : width + 16, :]
                units = dot(rows, fc[:width, :])
            else:
                rest = width - FC_CUT
                terms = far_b[rest : rest + 16, :]
                units = dot(rows[:, :FC_CUT], far_a[...]) + dot(rows[:, FC_CUT:], far_b[:rest, :])
            units = units + jnp.sum(terms.astype(jnp.float32), axis=0, keepdims=True)
            units = 0.5 * units * (1.0 + lax.erf(units * (0.5**0.5)))
            mean = dot(fours, units.astype(jnp.bfloat16)).astype(jnp.bfloat16)
            term = dot(mean, proj[lax.rem(x + step, shards)])
            total = term if total is None else total + term
        start = 0
        for _, count, out, done in parts:
            n = count // 4
            out[done : done + n, :] = total[start : start + n, :].astype(out.dtype)
            start += n


def pooled_parts(mine, other, weights, here, name):
    counts = (len(mine), len(other))
    rows_mine = sum(r.shape[0] for r in mine) // 4
    rows_other = sum(r.shape[0] for r in other) // 4
    width = mine[0].shape[1]
    units = weights[-1].shape[0] * weights[-1].shape[1]
    refs = [*mine, *other, *weights]
    flops = 2 * (rows_mine + rows_other) * 5 * width * units
    outs = (
        jax.ShapeDtypeStruct((rows_mine, width), jnp.float32),
        jax.ShapeDtypeStruct((rows_other, width), jnp.bfloat16),
    )
    return pl.pallas_call(
        lambda *r: mlp_kernel(counts, *r),
        out_shape=outs,
        in_specs=[pl.BlockSpec(memory_space=pltpu.SMEM)]
        + [pl.BlockSpec(memory_space=pltpu.VMEM) for _ in refs],
        out_specs=tuple(pl.BlockSpec(memory_space=pltpu.VMEM) for _ in outs),
        compiler_params=pltpu.CompilerParams(vmem_limit_bytes=24 << 20),
        cost_estimate=pl.CostEstimate(flops=flops, bytes_accessed=8 << 20, transcendentals=0),
        name=name,
    )(here, *refs)


def merge_kernel(
    own,
    other,
    from_low,
    from_high,
    from_far,
    mixed_mean,
    b_proj,
    gain,
    w_merge,
    b_merge,
    owner_col,
    owner_row,
    out,
):
    rows = own.shape[0]
    summed = own[...] + other[...].astype(jnp.float32)
    summed = summed + from_low[...].astype(jnp.float32)
    summed = summed + from_high[...].astype(jnp.float32)
    summed = summed + from_far[...].astype(jnp.float32)
    pooled = mixed_mean[...] + summed + b_proj[...]
    merge_in = layer_norm(pooled, gain[...]).astype(jnp.bfloat16)
    merged = (dot(merge_in, w_merge[...]) + b_merge[...]).astype(jnp.bfloat16)
    earlier = iota((rows, rows), 0) < iota((rows, rows), 1)
    same = owner_col[...] == owner_row[...]
    rank = jnp.sum(jnp.where(earlier & same, 1.0, 0.0), axis=0, keepdims=True).astype(jnp.int32)
    place = iota((out.shape[0], rows), 0)
    pick = (place // rows == owner_row[...]) & (place % rows == rank)
    out[...] = dot(jnp.where(pick, 1.0, 0.0).astype(jnp.bfloat16), merged).astype(jnp.bfloat16)


def attention(*args):
    rows, width = args[0].shape
    outs = (
        jax.ShapeDtypeStruct((rows, width), jnp.bfloat16),
        jax.ShapeDtypeStruct((rows // 4, width), jnp.float32),
    )
    return pl.pallas_call(
        attention_kernel,
        out_shape=outs,
        in_specs=[pl.BlockSpec(memory_space=pltpu.VMEM) for _ in args],
        out_specs=tuple(pl.BlockSpec(memory_space=pltpu.VMEM) for _ in outs),
        scratch_shapes=[pltpu.VMEM((rows, width), jnp.float32)],
        compiler_params=pltpu.CompilerParams(vmem_limit_bytes=16 << 20),
        cost_estimate=pl.CostEstimate(
            flops=24 * rows * rows * width, bytes_accessed=4 << 20, transcendentals=0
        ),
        name="attention",
    )(*args)


def body(
    stream,
    queries,
    key_cache,
    value_cache,
    segments,
    stale_rows,
    owners,
    attn_gain,
    w_key,
    key_bias,
    mlp_gain,
    w_fc,
    b_fc,
    w_proj,
    b_proj,
    merge_gain,
    w_merge,
    b_merge,
):
    row_count = stream.shape[0]
    model_width = stream.shape[1]
    tok_count = lax.axis_size("tok")
    x_count = lax.axis_size("x")
    tok = lax.axis_index("tok")
    here = lax.axis_index("x").astype(jnp.int32).reshape(1)
    units_here = w_fc.shape[1]

    below_values = passed_along(value_cache, 1)
    above_values = passed_along(value_cache, -1)

    local_rows = stale_rows % row_count
    listed = jnp.concatenate([local_rows, jnp.full((16 - local_rows.shape[0],), -1, jnp.int32)])
    refreshed = call(
        refresh_kernel,
        jax.ShapeDtypeStruct(key_cache.shape, jnp.bfloat16),
        "refresh",
        2 * 16 * model_width * model_width,
        16,
        stream,
        key_cache,
        listed[:, None],
        listed[None, :],
        attn_gain[None, :],
        w_key,
        key_bias[None, :],
    )
    below_keys = passed_along(refreshed, 1)
    above_keys = passed_along(refreshed, -1)

    fc_own = jnp.concatenate(
        [w_fc, three_terms(b_fc), jnp.zeros((13, units_here), jnp.bfloat16)], axis=0
    )
    fc_left = shift(fc_own, "x", 1)
    fc_right = shift(fc_own, "x", -1)
    fc_far_a = shift(fc_left[:FC_CUT], "x", 1)
    fc_far_b = shift(fc_right[FC_CUT:], "x", -1)
    proj_part = units_here // tok_count
    proj_piece = lax.dynamic_slice_in_dim(w_proj, tok * proj_part, proj_part, 0)
    proj_all = lax.all_gather(proj_piece, ("x", "tok"), axis=0, tiled=True)
    proj_all = proj_all.reshape(x_count, units_here, model_width)
    weights = (fc_own, fc_left, fc_right, fc_far_a, fc_far_b, proj_all)

    position = lax.axis_index(BLK)
    minus_ones = jnp.full((row_count,), -1, jnp.int32)
    seg_padded = jnp.concatenate([minus_ones, segments, minus_ones], axis=0)
    key_seg = lax.dynamic_slice_in_dim(seg_padded, position * row_count, 3 * row_count, 0)
    query_seg = lax.dynamic_slice_in_dim(segments, position * row_count, row_count, 0)
    merged_rows = row_count // 4
    m = merged_rows
    normed, mixed_mean = attention(
        queries,
        below_keys,
        refreshed,
        above_keys,
        below_values,
        value_cache,
        above_values,
        stream,
        query_seg[:, None],
        key_seg[None, :],
        mlp_gain[None, :],
    )

    half = row_count // 2
    z_low = shift(normed, "z", 1)
    z_high = shift(normed, "z", -1)
    swapped = shift(normed, "c", 1)
    near, near_sent = pooled_parts([normed], [swapped], weights, here, "mlp_near")
    z_far_a = shift(z_low[:half], "z", 1)
    z_far_b = shift(z_high[half:], "z", -1)
    z_low_other = shift(z_low, "c", 1)
    z_high_other = shift(z_high, "c", 1)
    next_to, next_sent = pooled_parts(
        [z_low, z_high], [z_low_other, z_high_other], weights, here, "mlp_next"
    )
    far_a_other = shift(z_far_a, "c", 1)
    far_b_other = shift(z_far_b, "c", 1)
    far, far_sent = pooled_parts(
        [z_far_a, z_far_b], [far_a_other, far_b_other], weights, here, "mlp_far"
    )

    near_other = shift(near_sent, "c", 1)
    next_other = shift(next_sent, "c", 1)
    next_sum = (next_to + next_other.astype(jnp.float32)).astype(jnp.bfloat16)
    from_high = shift(next_sum[:m], "z", -1)
    from_low = shift(next_sum[m:], "z", 1)
    far_other = shift(far_sent, "c", 1)
    far_sum = (far + far_other.astype(jnp.float32)).astype(jnp.bfloat16)
    from_far = shift(far_sum, "z", 2)
    outgoing = call(
        merge_kernel,
        jax.ShapeDtypeStruct((tok_count * m, model_width), jnp.bfloat16),
        "merge",
        2 * m * model_width * model_width,
        16,
        near,
        near_other,
        from_low,
        from_high,
        from_far,
        mixed_mean,
        b_proj[None, :],
        merge_gain[None, :],
        w_merge,
        b_merge[None, :],
        owners[:, None],
        owners[None, :],
    ).reshape(tok_count, m, model_width)
    arrived = lax.all_to_all(outgoing, "tok", split_axis=0, concat_axis=0, tiled=True)
    delivered = arrived.reshape(1, 1, tok_count * merged_rows, model_width)
    return (refreshed, delivered)


def solution(mesh):
    fine = Mesh(mesh.devices.reshape(4, 4, 2, 4), ("x", "z", "c", "tok"))
    return jax.shard_map(
        body,
        mesh=fine,
        in_specs=(
            P(ROWS, None),
            P(ROWS, None),
            P(ROWS, None),
            P(ROWS, None),
            P("tok"),
            P(ROWS),
            P(ROWS),
            P(),
            P(),
            P(),
            P(),
            P(None, BLK),
            P(BLK),
            P(BLK, None),
            P(),
            P(),
            P(),
            P(),
        ),
        out_specs=(P(ROWS, None), P("tok", BLK, None, None)),
        check_vma=False,
    )
```

```python
import jax
import jax.numpy as jnp
from jax import lax
from jax.experimental import pallas as pl
from jax.experimental.pallas import tpu as pltpu
from jax.sharding import Mesh
from jax.sharding import PartitionSpec as P

HEADS = 16
ROWS = ("tok", "x", "z", "c")
BLK = ("x", "z", "c")
FC_CUT = 768


def passed_along(block, distance):
    count = lax.axis_size("x") * lax.axis_size("z") * lax.axis_size("c")
    route = [(i - distance, i) for i in range(count) if 0 <= i - distance < count]
    return lax.ppermute(block, BLK, route)


def shift(block, axis, distance):
    count = lax.axis_size(axis)
    return lax.ppermute(block, axis, [(i, (i + distance) % count) for i in range(count)])


def after(value, *others):
    return lax.optimization_barrier((value, *others))[0]


def layer_norm(values, gain):
    center = values - jnp.mean(values, axis=-1, keepdims=True)
    spread = jnp.mean(center * center, axis=-1, keepdims=True)
    return center * lax.rsqrt(spread + 1e-06) * gain


def three_terms(values):
    high = values.astype(jnp.bfloat16)
    rest = values - high.astype(jnp.float32)
    middle = rest.astype(jnp.bfloat16)
    low = (rest - middle.astype(jnp.float32)).astype(jnp.bfloat16)
    return jnp.stack([high, middle, low])


def dot(left, right):
    return jnp.dot(left, right, preferred_element_type=jnp.float32)


def iota(shape, axis):
    return lax.broadcasted_iota(jnp.int32, shape, axis)


def mean_of_fours(rows):
    hit = iota((rows // 4, rows), 1) // 4 == iota((rows // 4, rows), 0)
    return jnp.where(hit, 0.25, 0.0).astype(jnp.bfloat16)


def column_of(row):
    count = row.shape[1]
    same = iota((count, count), 0) == iota((count, count), 1)
    wide = jnp.where(same, row.astype(jnp.float32), 0.0)
    return jnp.sum(wide, axis=1, keepdims=True).astype(jnp.int32)


class Fetch:
    def __init__(self, source, target, semaphore):
        self.copy = pltpu.make_async_copy(source, target, semaphore)
        self.copy.start()
        self.target = target

    def ref(self):
        if self.copy is not None:
            self.copy.wait()
            self.copy = None
        return self.target


def call(kernel, name, outs, flops, limit, fetched, direct=(), scalars=(), buffers=None, scratch=(), semaphores=None):
    n_s, n_f, n_d = len(scalars), len(fetched), len(direct)
    single = not isinstance(outs, tuple)
    n_o = 1 if single else len(outs)
    shapes = [pltpu.VMEM(a.shape, a.dtype) for a in fetched] if buffers is None else buffers

    def wrapped(*refs):
        scalar_refs = refs[:n_s]
        sources = refs[n_s : n_s + n_f]
        direct_refs = refs[n_s + n_f : n_s + n_f + n_d]
        out_refs = refs[n_s + n_f + n_d : n_s + n_f + n_d + n_o]
        rest = refs[n_s + n_f + n_d + n_o :]
        targets, semaphores, extra = rest[: len(shapes)], rest[len(shapes)], rest[len(shapes) + 1 :]
        kernel(scalar_refs, sources, targets, semaphores, direct_refs, out_refs, extra)

    moved = sum(a.size * a.dtype.itemsize for a in fetched)
    vmem = pl.BlockSpec(memory_space=pltpu.VMEM)
    return pl.pallas_call(
        wrapped,
        out_shape=outs,
        in_specs=[pl.BlockSpec(memory_space=pltpu.SMEM)] * n_s
        + [pl.BlockSpec(memory_space=pltpu.HBM)] * n_f
        + [vmem] * n_d,
        out_specs=vmem if single else tuple(vmem for _ in outs),
        scratch_shapes=[*shapes, pltpu.SemaphoreType.DMA((semaphores or len(shapes),)), *scratch],
        compiler_params=pltpu.CompilerParams(vmem_limit_bytes=60 << 20),
        cost_estimate=pl.CostEstimate(flops=flops, bytes_accessed=moved, transcendentals=0),
        name=name,
    )(*scalars, *fetched, *direct)


def fetch_all(sources, targets, semaphores):
    return [Fetch(s, t, semaphores.at[i]) for i, (s, t) in enumerate(zip(sources, targets))]


def refresh_kernel(_, sources, targets, semaphores, direct, outs, __):
    stream, keys, w_key = fetch_all(sources, targets, semaphores)
    listed, gain, key_bias = direct
    (out,) = outs
    block = keys.target.shape[0]
    rows = listed[...][None, :] % block
    place = jnp.where(rows == iota((block, rows.shape[1]), 0), 1.0, 0.0)
    hit = jnp.sum(place, axis=1, keepdims=True) > 0.5
    place = place.astype(jnp.bfloat16)
    picked = lax.dot_general(
        place, stream.ref()[...], (((0,), (0,)), ((), ())), preferred_element_type=jnp.float32
    )
    held = layer_norm(picked, gain[...][None, :]).astype(jnp.bfloat16)
    fresh = (dot(held, w_key.ref()[...]) + key_bias[...][None, :]).astype(jnp.bfloat16)
    spread = dot(place, fresh)
    old = keys.ref()[...].astype(jnp.float32)
    out[...] = jnp.where(hit, spread, old).astype(jnp.bfloat16)


def attention_kernel(scalars, sources, targets, semaphores, direct, outs, extra):
    fetches = fetch_all(sources, targets, semaphores)
    queries, keys_below, keys, keys_above, values_below, values, values_above, stream = fetches
    position = scalars[0][0]
    segments, gain = direct
    normed, mixed_mean = outs
    (attended,) = extra
    rows, width = queries.target.shape
    size = width // HEADS
    blocks = segments.shape[0]
    middle = segments[pl.ds(position, 1), :]
    before = segments[pl.ds(jnp.maximum(position - 1, 0), 1), :]
    behind = segments[pl.ds(jnp.minimum(position + 1, blocks - 1), 1), :]
    before = jnp.where(position > 0, before, -1)
    behind = jnp.where(position < blocks - 1, behind, -1)
    allowed = column_of(middle) == jnp.concatenate([before, middle, behind], axis=1)
    scale = 1.0 / size**0.5
    for h in range(HEADS):
        low = h * size // 128 * 128
        high = min(-(-(h + 1) * size // 128) * 128, width)
        lane = iota((1, high - low), 1) + low
        mine = (lane >= h * size) & (lane < (h + 1) * size)
        picked = jnp.where(mine, 1.0, 0.0).astype(jnp.bfloat16)
        query = queries.ref()[:, low:high] * picked
        key = jnp.concatenate(
            [k.ref()[:, low:high] for k in (keys_below, keys, keys_above)], axis=0
        )
        scores = lax.dot_general(
            query, key, (((1,), (1,)), ((), ())), preferred_element_type=jnp.float32
        )
        scores = jnp.where(allowed, scores * scale, -jnp.inf)
        weights = jnp.exp(scores - jnp.max(scores, axis=-1, keepdims=True))
        share = 1.0 / jnp.sum(weights, axis=-1, keepdims=True)
        value = jnp.concatenate(
            [v.ref()[:, low:high] for v in (values_below, values, values_above)], axis=0
        )
        found = dot((weights * share).astype(jnp.bfloat16), value)
        attended[:, low:high] = jnp.where(mine, found, attended[:, low:high])
    rounded = attended[...].astype(jnp.bfloat16)
    here = stream.ref()[...]
    fours = mean_of_fours(rows)
    mixed_mean[...] = dot(fours, here) + dot(fours, rounded)
    mixed = here.astype(jnp.float32) + rounded.astype(jnp.float32)
    normed[...] = layer_norm(mixed, gain[...][None, :]).astype(jnp.bfloat16)


def mlp_kernel(n_mine, n_other, scalars, sources, targets, semaphores, _, outs, __):
    x = scalars[0][0]
    n_rows = n_mine + n_other
    row_blocks = fetch_all(sources[:n_rows], targets[:n_rows], semaphores)
    gathered = sources[-1]
    shards, pieces, depth, width = gathered.shape
    depth = depth - 16
    fc, terms, proj = [], [], []
    at = n_rows
    units = targets[-1].shape[0]
    for number, step in enumerate((0, shards - 1, 1, 2)):
        shard = gathered.at[lax.rem(x + step, shards)]
        upper, lower = sources[n_rows + 2 * number : n_rows + 2 * number + 2]
        fc.append([Fetch(upper, targets[at], semaphores.at[at])])
        fc[-1].append(Fetch(lower, targets[at + 1], semaphores.at[at + 1]))
        terms.append(Fetch(shard.at[0, depth:, :units], targets[at + 2], semaphores.at[at + 2]))
        at += 3
    at_piece = at
    for number, step in enumerate((0, shards - 1, 1, 2)):
        shard = gathered.at[lax.rem(x + step, shards)]
        proj.append(
            [
                Fetch(
                    shard.at[piece, :depth, :],
                    targets[at].at[piece * depth : (piece + 1) * depth, :],
                    semaphores.at[at_piece + piece],
                )
                for piece in range(pieces)
            ]
        )
        at += 1
        at_piece += pieces
    if n_mine == 1:
        passes = [row_blocks]
    else:
        passes = [row_blocks[:n_mine], row_blocks[n_mine:]]
    for number, blocks in enumerate(passes):
        rows = jnp.concatenate([b.ref()[...] for b in blocks], axis=0)
        fours = mean_of_fours(rows.shape[0])
        total = None
        for (upper, lower), bias, projection, whole in zip(fc, terms, proj, targets[-shards:]):
            units = dot(rows[:, :FC_CUT], upper.ref()[...])
            units = units + dot(rows[:, FC_CUT:], lower.ref()[...])
            bias = jnp.sum(bias.ref()[...].astype(jnp.float32), axis=0, keepdims=True)
            units = units + bias
            units = 0.5 * units * (1.0 + lax.erf(units * (0.5**0.5)))
            mean = dot(fours, units.astype(jnp.bfloat16)).astype(jnp.bfloat16)
            for piece in projection:
                piece.ref()
            term = dot(mean, whole[...])
            total = term if total is None else total + term
        if len(passes) == 1:
            half = total.shape[0] // 2
            outs[0][...] = total[:half, :].astype(outs[0].dtype)
            outs[1][...] = total[half:, :].astype(outs[1].dtype)
        else:
            outs[number][...] = total.astype(outs[number].dtype)


def pooled_parts(mine, other, weights, here, name):
    rows, width = mine[0].shape
    *fc, proj = weights
    shards, pieces, _, _ = proj.shape
    units = fc[0].shape[1]
    fetched = [*mine, *other, *fc, proj]
    buffers = [pltpu.VMEM(a.shape, a.dtype) for a in (*mine, *other)]
    for number in range(shards):
        buffers += [pltpu.VMEM(a.shape, a.dtype) for a in fc[2 * number : 2 * number + 2]]
        buffers.append(pltpu.VMEM((16, units), proj.dtype))
    buffers += [pltpu.VMEM((units, width), proj.dtype)] * shards
    pooled_mine, pooled_other = len(mine) * rows // 4, len(other) * rows // 4
    return call(
        lambda *a: mlp_kernel(len(mine), len(other), *a),
        name,
        (
            jax.ShapeDtypeStruct((pooled_mine, width), jnp.float32),
            jax.ShapeDtypeStruct((pooled_other, width), jnp.bfloat16),
        ),
        2 * (pooled_mine + pooled_other) * 5 * width * units * shards,
        24,
        fetched,
        scalars=(here,),
        buffers=buffers,
        semaphores=len(buffers) + shards * pieces,
    )


def merge_kernel(_, sources, targets, semaphores, direct, outs, __):
    fetches = fetch_all(sources, targets, semaphores)
    parts, mixed_mean, w_merge = fetches[:5], fetches[5], fetches[6]
    b_proj, gain, b_merge, owners = direct
    (out,) = outs
    pooled = mixed_mean.ref()[...] + b_proj[...][None, :]
    for part in parts:
        pooled = pooled + part.ref()[...].astype(jnp.float32)
    rows = pooled.shape[0]
    merge_in = layer_norm(pooled, gain[...][None, :]).astype(jnp.bfloat16)
    merged = (dot(merge_in, w_merge.ref()[...]) + b_merge[...][None, :]).astype(jnp.bfloat16)
    owner = owners[...][None, :]
    earlier = iota((rows, rows), 0) < iota((rows, rows), 1)
    same = column_of(owner) == owner
    rank = jnp.sum(jnp.where(earlier & same, 1.0, 0.0), axis=0, keepdims=True).astype(jnp.int32)
    place = iota((out.shape[0], rows), 0)
    pick = (place // rows == owner) & (place % rows == rank)
    out[...] = dot(jnp.where(pick, 1.0, 0.0).astype(jnp.bfloat16), merged).astype(jnp.bfloat16)


def body(
    stream,
    queries,
    key_cache,
    value_cache,
    segments,
    stale_rows,
    owners,
    attn_gain,
    w_key,
    key_bias,
    mlp_gain,
    w_fc,
    b_fc,
    w_proj,
    b_proj,
    merge_gain,
    w_merge,
    b_merge,
):
    row_count = stream.shape[0]
    model_width = stream.shape[1]
    tok_count = lax.axis_size("tok")
    x_count = lax.axis_size("x")
    tok = lax.axis_index("tok")
    here = lax.axis_index("x").astype(jnp.int32).reshape(1)
    position = lax.axis_index(BLK).astype(jnp.int32).reshape(1)
    units_here = w_fc.shape[1]
    m = row_count // 4

    below_values = passed_along(value_cache, 1)
    above_values = passed_along(value_cache, -1)
    refreshed = call(
        refresh_kernel,
        "refresh",
        jax.ShapeDtypeStruct(key_cache.shape, jnp.bfloat16),
        2 * 16 * model_width * model_width,
        16,
        (stream, key_cache, w_key),
        (stale_rows, attn_gain, key_bias),
    )
    fc_a, fc_b = after(w_fc[:FC_CUT], stale_rows), w_fc[FC_CUT:]
    left_a = shift(fc_a, "x", 1)
    right_a = shift(fc_a, "x", -1)
    sent_keys = after(refreshed, below_values, above_values)
    below_keys = passed_along(sent_keys, 1)
    above_keys = passed_along(sent_keys, -1)
    sent_b = after(fc_b, below_keys, above_keys)
    left_b = shift(sent_b, "x", 1)
    right_b = shift(sent_b, "x", -1)
    far_a = shift(after(left_a, below_keys, above_keys), "x", 1)
    far_b = shift(right_b, "x", -1)
    proj_part = units_here // tok_count
    proj_piece = lax.dynamic_slice_in_dim(w_proj, tok * proj_part, proj_part, 0)
    terms = jnp.pad(three_terms(b_fc), ((0, 13), (0, model_width - units_here)))
    gathered = lax.all_gather(
        jnp.concatenate([proj_piece, terms], axis=0), ("x", "tok"), axis=0, tiled=False
    )
    gathered = gathered.reshape(x_count, tok_count, proj_part + 16, model_width)
    weights = (fc_a, fc_b, left_a, left_b, right_a, right_b, far_a, far_b, gathered)

    normed, mixed_mean = call(
        attention_kernel,
        "attention",
        (
            jax.ShapeDtypeStruct((row_count, model_width), jnp.bfloat16),
            jax.ShapeDtypeStruct((m, model_width), jnp.float32),
        ),
        24 * row_count * row_count * model_width,
        16,
        (
            queries,
            below_keys,
            refreshed,
            above_keys,
            below_values,
            value_cache,
            above_values,
            stream,
        ),
        (segments.reshape(-1, row_count), mlp_gain),
        scalars=(position,),
        scratch=(pltpu.VMEM((row_count, model_width), jnp.float32),),
    )

    z_low = shift(normed, "z", 1)
    z_high = shift(normed, "z", -1)
    z_far = shift(normed, "z", 2)
    swapped = shift(normed, "c", 1)
    near, near_sent = pooled_parts([normed], [swapped], weights, here, "mlp_near")
    z_low_other = shift(z_low, "c", 1)
    z_high_other = shift(z_high, "c", 1)
    next_to, next_sent = pooled_parts(
        [z_low, z_high], [z_low_other, z_high_other], weights, here, "mlp_next"
    )
    z_far_other = shift(z_far, "c", 1)
    far, far_sent = pooled_parts(
        [after(z_far, next_to)], [z_far_other], weights, here, "mlp_far"
    )

    near_other = shift(near_sent, "c", 1)
    next_other = shift(next_sent, "c", 1)
    next_sum = (next_to + next_other.astype(jnp.float32)).astype(jnp.bfloat16)
    from_high = shift(next_sum[:m], "z", -1)
    from_low = shift(next_sum[m:], "z", 1)
    far_other = shift(far_sent, "c", 1)
    far_sum = (far + far_other.astype(jnp.float32)).astype(jnp.bfloat16)
    from_far = shift(far_sum, "z", 2)
    outgoing = call(
        merge_kernel,
        "merge",
        jax.ShapeDtypeStruct((tok_count * m, model_width), jnp.bfloat16),
        2 * m * model_width * model_width,
        16,
        (near, near_other, from_low, from_high, from_far, mixed_mean, w_merge),
        (b_proj, merge_gain, b_merge, owners),
    ).reshape(tok_count, m, model_width)
    arrived = lax.all_to_all(outgoing, "tok", split_axis=0, concat_axis=0, tiled=True)
    delivered = arrived.reshape(1, 1, tok_count * m, model_width)
    return (refreshed, delivered)


def solution(mesh):
    fine = Mesh(mesh.devices.reshape(4, 4, 2, 4), ("x", "z", "c", "tok"))
    return jax.shard_map(
        body,
        mesh=fine,
        in_specs=(
            P(ROWS, None),
            P(ROWS, None),
            P(ROWS, None),
            P(ROWS, None),
            P("tok"),
            P(ROWS),
            P(ROWS),
            P(),
            P(),
            P(),
            P(),
            P(None, BLK),
            P(BLK),
            P(BLK, None),
            P(),
            P(),
            P(),
            P(),
        ),
        out_specs=(P(ROWS, None), P("tok", BLK, None, None)),
        check_vma=False,
    )
```

```python
import jax
import jax.numpy as jnp
from jax import lax
from jax.experimental import pallas as pl
from jax.experimental.pallas import tpu as pltpu
from jax.sharding import Mesh
from jax.sharding import PartitionSpec as P

HEADS = 16
ROWS = ("tok", "x", "z", "c")
BLK = ("x", "z", "c")
FC_CUT = 768


def passed_along(block, distance):
    count = lax.axis_size("x") * lax.axis_size("z") * lax.axis_size("c")
    route = [(i - distance, i) for i in range(count) if 0 <= i - distance < count]
    return lax.ppermute(block, BLK, route)


def shift(block, axis, distance):
    count = lax.axis_size(axis)
    return lax.ppermute(block, axis, [(i, (i + distance) % count) for i in range(count)])


def after(value, *others):
    return lax.optimization_barrier((value, *others))[0]


def layer_norm(values, gain):
    center = values - jnp.mean(values, axis=-1, keepdims=True)
    spread = jnp.mean(center * center, axis=-1, keepdims=True)
    return center * lax.rsqrt(spread + 1e-06) * gain


def three_terms(values):
    high = values.astype(jnp.bfloat16)
    rest = values - high.astype(jnp.float32)
    middle = rest.astype(jnp.bfloat16)
    low = (rest - middle.astype(jnp.float32)).astype(jnp.bfloat16)
    return jnp.stack([high, middle, low])


def dot(left, right):
    return jnp.dot(left, right, preferred_element_type=jnp.float32)


def iota(shape, axis):
    return lax.broadcasted_iota(jnp.int32, shape, axis)


def mean_of_fours(rows):
    hit = iota((rows // 4, rows), 1) // 4 == iota((rows // 4, rows), 0)
    return jnp.where(hit, 0.25, 0.0).astype(jnp.bfloat16)


def column_of(row):
    count = row.shape[1]
    same = iota((count, count), 0) == iota((count, count), 1)
    wide = jnp.where(same, row.astype(jnp.float32), 0.0)
    return jnp.sum(wide, axis=1, keepdims=True).astype(jnp.int32)


class Fetch:
    def __init__(self, source, target, semaphore):
        self.copy = pltpu.make_async_copy(source, target, semaphore)
        self.copy.start()
        self.target = target

    def ref(self):
        if self.copy is not None:
            self.copy.wait()
            self.copy = None
        return self.target


def call(kernel, name, outs, flops, limit, fetched, direct=(), scalars=(), buffers=None, scratch=(), semaphores=None):
    n_s, n_f, n_d = len(scalars), len(fetched), len(direct)
    single = not isinstance(outs, tuple)
    n_o = 1 if single else len(outs)
    shapes = [pltpu.VMEM(a.shape, a.dtype) for a in fetched] if buffers is None else buffers

    def wrapped(*refs):
        scalar_refs = refs[:n_s]
        sources = refs[n_s : n_s + n_f]
        direct_refs = refs[n_s + n_f : n_s + n_f + n_d]
        out_refs = refs[n_s + n_f + n_d : n_s + n_f + n_d + n_o]
        rest = refs[n_s + n_f + n_d + n_o :]
        targets, semaphores, extra = rest[: len(shapes)], rest[len(shapes)], rest[len(shapes) + 1 :]
        kernel(scalar_refs, sources, targets, semaphores, direct_refs, out_refs, extra)

    moved = sum(a.size * a.dtype.itemsize for a in fetched)
    vmem = pl.BlockSpec(memory_space=pltpu.VMEM)
    return pl.pallas_call(
        wrapped,
        out_shape=outs,
        in_specs=[pl.BlockSpec(memory_space=pltpu.SMEM)] * n_s
        + [pl.BlockSpec(memory_space=pltpu.HBM)] * n_f
        + [vmem] * n_d,
        out_specs=vmem if single else tuple(vmem for _ in outs),
        scratch_shapes=[*shapes, pltpu.SemaphoreType.DMA((semaphores or len(shapes),)), *scratch],
        compiler_params=pltpu.CompilerParams(vmem_limit_bytes=60 << 20),
        cost_estimate=pl.CostEstimate(flops=flops, bytes_accessed=moved, transcendentals=0),
        name=name,
    )(*scalars, *fetched, *direct)


def fetch_all(sources, targets, semaphores):
    return [Fetch(s, t, semaphores.at[i]) for i, (s, t) in enumerate(zip(sources, targets))]


def refresh_kernel(_, sources, targets, semaphores, direct, outs, __):
    stream, keys, w_key = fetch_all(sources, targets, semaphores)
    listed, gain, key_bias = direct
    (out,) = outs
    block = keys.target.shape[0]
    rows = listed[...][None, :] % block
    place = jnp.where(rows == iota((block, rows.shape[1]), 0), 1.0, 0.0)
    hit = jnp.sum(place, axis=1, keepdims=True) > 0.5
    place = place.astype(jnp.bfloat16)
    picked = lax.dot_general(
        place, stream.ref()[...], (((0,), (0,)), ((), ())), preferred_element_type=jnp.float32
    )
    held = layer_norm(picked, gain[...][None, :]).astype(jnp.bfloat16)
    fresh = (dot(held, w_key.ref()[...]) + key_bias[...][None, :]).astype(jnp.bfloat16)
    spread = dot(place, fresh)
    old = keys.ref()[...].astype(jnp.float32)
    out[...] = jnp.where(hit, spread, old).astype(jnp.bfloat16)


def attention_kernel(scalars, sources, targets, semaphores, direct, outs, extra):
    fetches = fetch_all(sources, targets, semaphores)
    queries, keys_below, keys, keys_above, values_below, values, values_above, stream = fetches
    position = scalars[0][0]
    segments, gain = direct
    normed, mixed_mean = outs
    (attended,) = extra
    rows, width = queries.target.shape
    size = width // HEADS
    blocks = segments.shape[0]
    middle = segments[pl.ds(position, 1), :]
    before = segments[pl.ds(jnp.maximum(position - 1, 0), 1), :]
    behind = segments[pl.ds(jnp.minimum(position + 1, blocks - 1), 1), :]
    before = jnp.where(position > 0, before, -1)
    behind = jnp.where(position < blocks - 1, behind, -1)
    allowed = column_of(middle) == jnp.concatenate([before, middle, behind], axis=1)
    scale = 1.0 / size**0.5
    for h in range(HEADS):
        low = h * size // 128 * 128
        high = min(-(-(h + 1) * size // 128) * 128, width)
        lane = iota((1, high - low), 1) + low
        mine = (lane >= h * size) & (lane < (h + 1) * size)
        picked = jnp.where(mine, 1.0, 0.0).astype(jnp.bfloat16)
        query = queries.ref()[:, low:high] * picked
        key = jnp.concatenate(
            [k.ref()[:, low:high] for k in (keys_below, keys, keys_above)], axis=0
        )
        scores = lax.dot_general(
            query, key, (((1,), (1,)), ((), ())), preferred_element_type=jnp.float32
        )
        scores = jnp.where(allowed, scores * scale, -jnp.inf)
        weights = jnp.exp(scores - jnp.max(scores, axis=-1, keepdims=True))
        share = 1.0 / jnp.sum(weights, axis=-1, keepdims=True)
        value = jnp.concatenate(
            [v.ref()[:, low:high] for v in (values_below, values, values_above)], axis=0
        )
        found = dot((weights * share).astype(jnp.bfloat16), value)
        attended[:, low:high] = jnp.where(mine, found, attended[:, low:high])
    rounded = attended[...].astype(jnp.bfloat16)
    here = stream.ref()[...]
    fours = mean_of_fours(rows)
    mixed_mean[...] = dot(fours, here) + dot(fours, rounded)
    mixed = here.astype(jnp.float32) + rounded.astype(jnp.float32)
    normed[...] = layer_norm(mixed, gain[...][None, :]).astype(jnp.bfloat16)


def mlp_kernel(n_mine, n_other, scalars, sources, targets, semaphores, _, outs, __):
    x = scalars[0][0]
    n_rows = n_mine + n_other
    row_blocks = fetch_all(sources[:n_rows], targets[:n_rows], semaphores)
    gathered = sources[-1]
    shards, pieces, depth, width = gathered.shape
    depth = depth - 16
    fc, terms, proj = [], [], []
    at = n_rows
    units = targets[-1].shape[0]
    for number, step in enumerate((0, shards - 1, 1, 2)):
        shard = gathered.at[lax.rem(x + step, shards)]
        upper, lower = sources[n_rows + 2 * number : n_rows + 2 * number + 2]
        fc.append([Fetch(upper, targets[at], semaphores.at[at])])
        fc[-1].append(Fetch(lower, targets[at + 1], semaphores.at[at + 1]))
        terms.append(Fetch(shard.at[0, depth:, :units], targets[at + 2], semaphores.at[at + 2]))
        at += 3
    at_piece = at
    for number, step in enumerate((0, shards - 1, 1, 2)):
        shard = gathered.at[lax.rem(x + step, shards)]
        proj.append(
            [
                Fetch(
                    shard.at[piece, :depth, :],
                    targets[at].at[piece * depth : (piece + 1) * depth, :],
                    semaphores.at[at_piece + piece],
                )
                for piece in range(pieces)
            ]
        )
        at += 1
        at_piece += pieces
    passes = [
        (out, first // 2, row_blocks[base + first : base + first + 2])
        for out, base, count in ((outs[0], 0, n_mine), (outs[1], n_mine, n_other))
        for first in range(0, count, 2)
    ]
    for out, number, blocks in passes:
        rows = jnp.concatenate([b.ref()[...] for b in blocks], axis=0)
        fours = mean_of_fours(rows.shape[0])
        total = None
        for (upper, lower), bias, projection, whole in zip(fc, terms, proj, targets[-shards:]):
            units = dot(rows[:, :FC_CUT], upper.ref()[...])
            units = units + dot(rows[:, FC_CUT:], lower.ref()[...])
            bias = jnp.sum(bias.ref()[...].astype(jnp.float32), axis=0, keepdims=True)
            units = units + bias
            units = 0.5 * units * (1.0 + lax.erf(units * (0.5**0.5)))
            mean = dot(fours, units.astype(jnp.bfloat16)).astype(jnp.bfloat16)
            for piece in projection:
                piece.ref()
            term = dot(mean, whole[...])
            total = term if total is None else total + term
        count = total.shape[0]
        out[number * count : (number + 1) * count, :] = total.astype(out.dtype)


def pooled_parts(mine, other, weights, here, name):
    rows, width = mine[0].shape
    *fc, proj = weights
    shards, pieces, _, _ = proj.shape
    units = fc[0].shape[1]
    fetched = [*mine, *other, *fc, proj]
    buffers = [pltpu.VMEM(a.shape, a.dtype) for a in (*mine, *other)]
    for number in range(shards):
        buffers += [pltpu.VMEM(a.shape, a.dtype) for a in fc[2 * number : 2 * number + 2]]
        buffers.append(pltpu.VMEM((16, units), proj.dtype))
    buffers += [pltpu.VMEM((units, width), proj.dtype)] * shards
    pooled_mine, pooled_other = len(mine) * rows // 4, len(other) * rows // 4
    return call(
        lambda *a: mlp_kernel(len(mine), len(other), *a),
        name,
        (
            jax.ShapeDtypeStruct((pooled_mine, width), jnp.float32),
            jax.ShapeDtypeStruct((pooled_other, width), jnp.bfloat16),
        ),
        2 * (pooled_mine + pooled_other) * 5 * width * units * shards,
        24,
        fetched,
        scalars=(here,),
        buffers=buffers,
        semaphores=len(buffers) + shards * pieces,
    )


def merge_kernel(_, sources, targets, semaphores, direct, outs, __):
    fetches = fetch_all(sources[:5], targets, semaphores)
    w_source = sources[5]
    parts, mixed_mean = fetches[:4], fetches[4]
    depth = w_source.shape[0]
    cuts = [(low, min(low + 512, depth)) for low in range(0, depth, 512)]
    w_merge = [
        Fetch(
            w_source.at[low:high, :], targets[5].at[low:high, :], semaphores.at[5 + i]
        )
        for i, (low, high) in enumerate(cuts)
    ]
    b_proj, gain, b_merge, owners = direct
    (out,) = outs
    pooled = mixed_mean.ref()[...] + b_proj[...][None, :]
    for part in parts:
        pooled = pooled + part.ref()[...].astype(jnp.float32)
    rows = pooled.shape[0]
    merge_in = layer_norm(pooled, gain[...][None, :]).astype(jnp.bfloat16)
    merged = b_merge[...][None, :]
    for (low, high), fetch in zip(cuts, w_merge):
        merged = merged + dot(merge_in[:, low:high], fetch.ref()[...])
    merged = merged.astype(jnp.bfloat16)
    owner = owners[...][None, :]
    earlier = iota((rows, rows), 0) < iota((rows, rows), 1)
    same = column_of(owner) == owner
    rank = jnp.sum(jnp.where(earlier & same, 1.0, 0.0), axis=0, keepdims=True).astype(jnp.int32)
    place = iota((out.shape[0], rows), 0)
    pick = (place // rows == owner) & (place % rows == rank)
    out[...] = dot(jnp.where(pick, 1.0, 0.0).astype(jnp.bfloat16), merged).astype(jnp.bfloat16)


def body(
    stream,
    queries,
    key_cache,
    value_cache,
    segments,
    stale_rows,
    owners,
    attn_gain,
    w_key,
    key_bias,
    mlp_gain,
    w_fc,
    b_fc,
    w_proj,
    b_proj,
    merge_gain,
    w_merge,
    b_merge,
):
    row_count = stream.shape[0]
    model_width = stream.shape[1]
    tok_count = lax.axis_size("tok")
    x_count = lax.axis_size("x")
    tok = lax.axis_index("tok")
    here = lax.axis_index("x").astype(jnp.int32).reshape(1)
    position = lax.axis_index(BLK).astype(jnp.int32).reshape(1)
    units_here = w_fc.shape[1]
    m = row_count // 4

    below_values = passed_along(value_cache, 1)
    above_values = passed_along(value_cache, -1)
    refreshed = call(
        refresh_kernel,
        "refresh",
        jax.ShapeDtypeStruct(key_cache.shape, jnp.bfloat16),
        2 * 16 * model_width * model_width,
        16,
        (stream, key_cache, w_key),
        (stale_rows, attn_gain, key_bias),
    )
    fc_a, fc_b = after(w_fc[:FC_CUT], stale_rows), w_fc[FC_CUT:]
    left_a = shift(fc_a, "x", 1)
    right_a = shift(fc_a, "x", -1)
    sent_keys = after(refreshed, below_values, above_values)
    below_keys = passed_along(sent_keys, 1)
    above_keys = passed_along(sent_keys, -1)
    sent_b = after(fc_b, below_keys, above_keys)
    left_b = shift(sent_b, "x", 1)
    right_b = shift(sent_b, "x", -1)
    far_a = shift(left_a, "x", 1)
    far_b = shift(right_b, "x", -1)
    proj_part = units_here // tok_count
    proj_piece = lax.dynamic_slice_in_dim(w_proj, tok * proj_part, proj_part, 0)
    terms = jnp.pad(three_terms(b_fc), ((0, 13), (0, model_width - units_here)))
    gathered = lax.all_gather(
        jnp.concatenate([proj_piece, terms], axis=0), ("x", "tok"), axis=0, tiled=False
    )
    gathered = gathered.reshape(x_count, tok_count, proj_part + 16, model_width)
    weights = (fc_a, fc_b, left_a, left_b, right_a, right_b, far_a, far_b, gathered)

    normed, mixed_mean = call(
        attention_kernel,
        "attention",
        (
            jax.ShapeDtypeStruct((row_count, model_width), jnp.bfloat16),
            jax.ShapeDtypeStruct((m, model_width), jnp.float32),
        ),
        24 * row_count * row_count * model_width,
        16,
        (
            queries,
            below_keys,
            refreshed,
            above_keys,
            below_values,
            value_cache,
            above_values,
            stream,
        ),
        (segments.reshape(-1, row_count), mlp_gain),
        scalars=(position,),
        scratch=(pltpu.VMEM((row_count, model_width), jnp.float32),),
    )

    z_low = shift(normed, "z", 1)
    z_high = shift(normed, "z", -1)
    z_far = shift(normed, "z", 2)
    swapped = shift(normed, "c", 1)
    z_low_other = shift(z_low, "c", 1)
    z_high_other = shift(z_high, "c", 1)
    z_far_other = shift(z_far, "c", 1)
    mine, sent = pooled_parts(
        [normed, z_low, z_high, z_far],
        [swapped, z_low_other, z_high_other, z_far_other],
        weights,
        here,
        "mlp",
    )

    sums = mine + shift(sent, "c", 1).astype(jnp.float32)
    own = sums[:m]
    from_high = shift(sums[m : 2 * m].astype(jnp.bfloat16), "z", -1)
    from_low = shift(sums[2 * m : 3 * m].astype(jnp.bfloat16), "z", 1)
    from_far = shift(sums[3 * m :].astype(jnp.bfloat16), "z", 2)
    outgoing = call(
        merge_kernel,
        "merge",
        jax.ShapeDtypeStruct((tok_count * m, model_width), jnp.bfloat16),
        2 * m * model_width * model_width,
        16,
        (own, from_low, from_high, from_far, mixed_mean, w_merge),
        (b_proj, merge_gain, b_merge, owners),
        semaphores=9,
    ).reshape(tok_count, m, model_width)
    arrived = lax.all_to_all(outgoing, "tok", split_axis=0, concat_axis=0, tiled=True)
    delivered = arrived.reshape(1, 1, tok_count * m, model_width)
    return (refreshed, delivered)


def solution(mesh):
    fine = Mesh(mesh.devices.reshape(4, 4, 2, 4), ("x", "z", "c", "tok"))
    return jax.shard_map(
        body,
        mesh=fine,
        in_specs=(
            P(ROWS, None),
            P(ROWS, None),
            P(ROWS, None),
            P(ROWS, None),
            P("tok"),
            P(ROWS),
            P(ROWS),
            P(),
            P(),
            P(),
            P(),
            P(None, BLK),
            P(BLK),
            P(BLK, None),
            P(),
            P(),
            P(),
            P(),
        ),
        out_specs=(P(ROWS, None), P("tok", BLK, None, None)),
        check_vma=False,
    )
```

```python
import jax
import jax.numpy as jnp
from jax import lax
from jax.experimental import pallas as pl
from jax.experimental.pallas import tpu as pltpu
from jax.sharding import Mesh
from jax.sharding import PartitionSpec as P

HEADS = 16
ROWS = ("tok", "x", "z", "c")
BLK = ("x", "z", "c")
FC_CUT = 768


def passed_along(block, distance):
    count = lax.axis_size("x") * lax.axis_size("z") * lax.axis_size("c")
    route = [(i - distance, i) for i in range(count) if 0 <= i - distance < count]
    return lax.ppermute(block, BLK, route)


def shift(block, axis, distance):
    count = lax.axis_size(axis)
    return lax.ppermute(block, axis, [(i, (i + distance) % count) for i in range(count)])


def after(value, *others):
    return lax.optimization_barrier((value, *others))[0]


def layer_norm(values, gain):
    center = values - jnp.mean(values, axis=-1, keepdims=True)
    spread = jnp.mean(center * center, axis=-1, keepdims=True)
    return center * lax.rsqrt(spread + 1e-06) * gain


def three_terms(values):
    high = values.astype(jnp.bfloat16)
    rest = values - high.astype(jnp.float32)
    middle = rest.astype(jnp.bfloat16)
    low = (rest - middle.astype(jnp.float32)).astype(jnp.bfloat16)
    return jnp.stack([high, middle, low])


def dot(left, right):
    return jnp.dot(left, right, preferred_element_type=jnp.float32)


def iota(shape, axis):
    return lax.broadcasted_iota(jnp.int32, shape, axis)


def mean_of_fours(rows):
    hit = iota((rows // 4, rows), 1) // 4 == iota((rows // 4, rows), 0)
    return jnp.where(hit, 0.25, 0.0).astype(jnp.bfloat16)


def column_of(row):
    count = row.shape[1]
    same = iota((count, count), 0) == iota((count, count), 1)
    wide = jnp.where(same, row.astype(jnp.float32), 0.0)
    return jnp.sum(wide, axis=1, keepdims=True).astype(jnp.int32)


class Fetch:
    def __init__(self, source, target, semaphore):
        self.copy = pltpu.make_async_copy(source, target, semaphore)
        self.copy.start()
        self.target = target

    def ref(self):
        if self.copy is not None:
            self.copy.wait()
            self.copy = None
        return self.target


def call(kernel, name, outs, flops, limit, fetched, direct=(), scalars=(), buffers=None, scratch=(), semaphores=None):
    n_s, n_f, n_d = len(scalars), len(fetched), len(direct)
    single = not isinstance(outs, tuple)
    n_o = 1 if single else len(outs)
    shapes = [pltpu.VMEM(a.shape, a.dtype) for a in fetched] if buffers is None else buffers

    def wrapped(*refs):
        scalar_refs = refs[:n_s]
        sources = refs[n_s : n_s + n_f]
        direct_refs = refs[n_s + n_f : n_s + n_f + n_d]
        out_refs = refs[n_s + n_f + n_d : n_s + n_f + n_d + n_o]
        rest = refs[n_s + n_f + n_d + n_o :]
        targets, semaphores, extra = rest[: len(shapes)], rest[len(shapes)], rest[len(shapes) + 1 :]
        kernel(scalar_refs, sources, targets, semaphores, direct_refs, out_refs, extra)

    moved = sum(a.size * a.dtype.itemsize for a in fetched)
    vmem = pl.BlockSpec(memory_space=pltpu.VMEM)
    return pl.pallas_call(
        wrapped,
        out_shape=outs,
        in_specs=[pl.BlockSpec(memory_space=pltpu.SMEM)] * n_s
        + [pl.BlockSpec(memory_space=pltpu.HBM)] * n_f
        + [vmem] * n_d,
        out_specs=vmem if single else tuple(vmem for _ in outs),
        scratch_shapes=[*shapes, pltpu.SemaphoreType.DMA((semaphores or len(shapes),)), *scratch],
        compiler_params=pltpu.CompilerParams(vmem_limit_bytes=60 << 20),
        cost_estimate=pl.CostEstimate(flops=flops, bytes_accessed=moved, transcendentals=0),
        name=name,
    )(*scalars, *fetched, *direct)


def fetch_all(sources, targets, semaphores):
    return [Fetch(s, t, semaphores.at[i]) for i, (s, t) in enumerate(zip(sources, targets))]


def refresh_kernel(_, sources, targets, semaphores, direct, outs, __):
    stream, keys, w_key = fetch_all(sources, targets, semaphores)
    listed, gain, key_bias = direct
    (out,) = outs
    block = keys.target.shape[0]
    rows = listed[...][None, :] % block
    place = jnp.where(rows == iota((block, rows.shape[1]), 0), 1.0, 0.0)
    hit = jnp.sum(place, axis=1, keepdims=True) > 0.5
    place = place.astype(jnp.bfloat16)
    picked = lax.dot_general(
        place, stream.ref()[...], (((0,), (0,)), ((), ())), preferred_element_type=jnp.float32
    )
    held = layer_norm(picked, gain[...][None, :]).astype(jnp.bfloat16)
    fresh = (dot(held, w_key.ref()[...]) + key_bias[...][None, :]).astype(jnp.bfloat16)
    spread = dot(place, fresh)
    old = keys.ref()[...].astype(jnp.float32)
    out[...] = jnp.where(hit, spread, old).astype(jnp.bfloat16)


def attention_kernel(scalars, sources, targets, semaphores, direct, outs, extra):
    fetches = fetch_all(sources, targets, semaphores)
    queries, keys_below, keys, keys_above, values_below, values, values_above, stream = fetches
    position = scalars[0][0]
    segments, gain = direct
    normed, mixed_mean = outs
    (attended,) = extra
    rows, width = queries.target.shape
    size = width // HEADS
    blocks = segments.shape[0]
    middle = segments[pl.ds(position, 1), :]
    before = segments[pl.ds(jnp.maximum(position - 1, 0), 1), :]
    behind = segments[pl.ds(jnp.minimum(position + 1, blocks - 1), 1), :]
    before = jnp.where(position > 0, before, -1)
    behind = jnp.where(position < blocks - 1, behind, -1)
    allowed = column_of(middle) == jnp.concatenate([before, middle, behind], axis=1)
    scale = 1.0 / size**0.5
    for h in range(HEADS):
        low = h * size // 128 * 128
        high = min(-(-(h + 1) * size // 128) * 128, width)
        lane = iota((1, high - low), 1) + low
        mine = (lane >= h * size) & (lane < (h + 1) * size)
        picked = jnp.where(mine, 1.0, 0.0).astype(jnp.bfloat16)
        query = queries.ref()[:, low:high] * picked
        key = jnp.concatenate(
            [k.ref()[:, low:high] for k in (keys_below, keys, keys_above)], axis=0
        )
        scores = lax.dot_general(
            query, key, (((1,), (1,)), ((), ())), preferred_element_type=jnp.float32
        )
        scores = jnp.where(allowed, scores * scale, -jnp.inf)
        weights = jnp.exp(scores - jnp.max(scores, axis=-1, keepdims=True))
        share = 1.0 / jnp.sum(weights, axis=-1, keepdims=True)
        value = jnp.concatenate(
            [v.ref()[:, low:high] for v in (values_below, values, values_above)], axis=0
        )
        found = dot((weights * share).astype(jnp.bfloat16), value)
        attended[:, low:high] = jnp.where(mine, found, attended[:, low:high])
    rounded = attended[...].astype(jnp.bfloat16)
    here = stream.ref()[...]
    fours = mean_of_fours(rows)
    mixed_mean[...] = dot(fours, here) + dot(fours, rounded)
    mixed = here.astype(jnp.float32) + rounded.astype(jnp.float32)
    normed[...] = layer_norm(mixed, gain[...][None, :]).astype(jnp.bfloat16)


def mlp_kernel(n_mine, n_other, scalars, sources, targets, semaphores, _, outs, __):
    x = scalars[0][0]
    n_rows = n_mine + n_other
    row_blocks = fetch_all(sources[:n_rows], targets[:n_rows], semaphores)
    gathered = sources[-1]
    shards, pieces, depth, width = gathered.shape
    depth = depth - 8
    fc, terms, proj = [], [], []
    at = n_rows
    units = targets[-1].shape[0]
    for number, step in enumerate((0, shards - 1, 1, 2)):
        shard = gathered.at[lax.rem(x + step, shards)]
        upper, lower = sources[n_rows + 2 * number : n_rows + 2 * number + 2]
        fc.append([Fetch(upper, targets[at], semaphores.at[at])])
        fc[-1].append(Fetch(lower, targets[at + 1], semaphores.at[at + 1]))
        terms.append(Fetch(shard.at[0, depth:, :units], targets[at + 2], semaphores.at[at + 2]))
        at += 3
    at_piece = at
    for number, step in enumerate((0, shards - 1, 1, 2)):
        shard = gathered.at[lax.rem(x + step, shards)]
        proj.append(
            [
                Fetch(
                    shard.at[piece, :depth, :],
                    targets[at].at[piece * depth : (piece + 1) * depth, :],
                    semaphores.at[at_piece + piece],
                )
                for piece in range(pieces)
            ]
        )
        at += 1
        at_piece += pieces
    passes = [
        (out, first // 2, row_blocks[base + first : base + first + 2])
        for out, base, count in ((outs[0], 0, n_mine), (outs[1], n_mine, n_other))
        for first in range(0, count, 2)
    ]
    for out, number, blocks in passes:
        rows = jnp.concatenate([b.ref()[...] for b in blocks], axis=0)
        fours = mean_of_fours(rows.shape[0])
        total = None
        for (upper, lower), bias, projection, whole in zip(fc, terms, proj, targets[-shards:]):
            units = dot(rows[:, :FC_CUT], upper.ref()[...])
            units = units + dot(rows[:, FC_CUT:], lower.ref()[...])
            bias = jnp.sum(bias.ref()[...].astype(jnp.float32), axis=0, keepdims=True)
            units = units + bias
            units = 0.5 * units * (1.0 + lax.erf(units * (0.5**0.5)))
            mean = dot(fours, units.astype(jnp.bfloat16)).astype(jnp.bfloat16)
            for piece in projection:
                piece.ref()
            term = dot(mean, whole[...])
            total = term if total is None else total + term
        count = total.shape[0]
        out[number * count : (number + 1) * count, :] = total.astype(out.dtype)


def pooled_parts(mine, other, weights, here, name):
    rows, width = mine[0].shape
    *fc, proj = weights
    shards, pieces, _, _ = proj.shape
    units = fc[0].shape[1]
    fetched = [*mine, *other, *fc, proj]
    buffers = [pltpu.VMEM(a.shape, a.dtype) for a in (*mine, *other)]
    for number in range(shards):
        buffers += [pltpu.VMEM(a.shape, a.dtype) for a in fc[2 * number : 2 * number + 2]]
        buffers.append(pltpu.VMEM((8, units), proj.dtype))
    buffers += [pltpu.VMEM((units, width), proj.dtype)] * shards
    pooled_mine, pooled_other = len(mine) * rows // 4, len(other) * rows // 4
    return call(
        lambda *a: mlp_kernel(len(mine), len(other), *a),
        name,
        (
            jax.ShapeDtypeStruct((pooled_mine, width), jnp.float32),
            jax.ShapeDtypeStruct((pooled_other, width), jnp.bfloat16),
        ),
        2 * (pooled_mine + pooled_other) * 5 * width * units * shards,
        24,
        fetched,
        scalars=(here,),
        buffers=buffers,
        semaphores=len(buffers) + shards * pieces,
    )


def merge_kernel(_, sources, targets, semaphores, direct, outs, __):
    fetches = fetch_all(sources[:5], targets, semaphores)
    w_source = sources[5]
    parts, mixed_mean = fetches[:4], fetches[4]
    depth = w_source.shape[0]
    cuts = [(low, min(low + 512, depth)) for low in range(0, depth, 512)]
    w_merge = [
        Fetch(
            w_source.at[low:high, :], targets[5].at[low:high, :], semaphores.at[5 + i]
        )
        for i, (low, high) in enumerate(cuts)
    ]
    b_proj, gain, b_merge, owners = direct
    (out,) = outs
    pooled = mixed_mean.ref()[...] + b_proj[...][None, :]
    for part in parts:
        pooled = pooled + part.ref()[...].astype(jnp.float32)
    rows = pooled.shape[0]
    merge_in = layer_norm(pooled, gain[...][None, :]).astype(jnp.bfloat16)
    merged = b_merge[...][None, :]
    for (low, high), fetch in zip(cuts, w_merge):
        merged = merged + dot(merge_in[:, low:high], fetch.ref()[...])
    merged = merged.astype(jnp.bfloat16)
    owner = owners[...][None, :]
    earlier = iota((rows, rows), 0) < iota((rows, rows), 1)
    same = column_of(owner) == owner
    rank = jnp.sum(jnp.where(earlier & same, 1.0, 0.0), axis=0, keepdims=True).astype(jnp.int32)
    place = iota((out.shape[0], rows), 0)
    pick = (place // rows == owner) & (place % rows == rank)
    out[...] = dot(jnp.where(pick, 1.0, 0.0).astype(jnp.bfloat16), merged).astype(jnp.bfloat16)


def body(
    stream,
    queries,
    key_cache,
    value_cache,
    segments,
    stale_rows,
    owners,
    attn_gain,
    w_key,
    key_bias,
    mlp_gain,
    w_fc,
    b_fc,
    w_proj,
    b_proj,
    merge_gain,
    w_merge,
    b_merge,
):
    row_count = stream.shape[0]
    model_width = stream.shape[1]
    tok_count = lax.axis_size("tok")
    x_count = lax.axis_size("x")
    tok = lax.axis_index("tok")
    here = lax.axis_index("x").astype(jnp.int32).reshape(1)
    position = lax.axis_index(BLK).astype(jnp.int32).reshape(1)
    units_here = w_fc.shape[1]
    m = row_count // 4

    below_values = passed_along(value_cache, 1)
    above_values = passed_along(value_cache, -1)
    refreshed = call(
        refresh_kernel,
        "refresh",
        jax.ShapeDtypeStruct(key_cache.shape, jnp.bfloat16),
        2 * 16 * model_width * model_width,
        16,
        (stream, key_cache, w_key),
        (stale_rows, attn_gain, key_bias),
    )
    fc_a, fc_b = after(w_fc[:FC_CUT], stale_rows), w_fc[FC_CUT:]
    left_a = shift(fc_a, "x", 1)
    right_a = shift(fc_a, "x", -1)
    sent_keys = after(refreshed, below_values, above_values)
    below_keys = passed_along(sent_keys, 1)
    above_keys = passed_along(sent_keys, -1)
    sent_b = after(fc_b, below_keys, above_keys)
    left_b = shift(sent_b, "x", 1)
    right_b = shift(sent_b, "x", -1)
    far_a = shift(left_a, "x", 1)
    far_b = shift(right_b, "x", -1)
    proj_part = units_here // tok_count
    proj_piece = lax.dynamic_slice_in_dim(w_proj, tok * proj_part, proj_part, 0)
    terms = jnp.pad(three_terms(b_fc), ((0, 5), (0, model_width - units_here)))
    gathered = lax.all_gather(
        jnp.concatenate([proj_piece, terms], axis=0), ("x", "tok"), axis=0, tiled=False
    )
    gathered = gathered.reshape(x_count, tok_count, proj_part + 8, model_width)
    weights = (fc_a, fc_b, left_a, left_b, right_a, right_b, far_a, far_b, gathered)

    normed, mixed_mean = call(
        attention_kernel,
        "attention",
        (
            jax.ShapeDtypeStruct((row_count, model_width), jnp.bfloat16),
            jax.ShapeDtypeStruct((m, model_width), jnp.float32),
        ),
        24 * row_count * row_count * model_width,
        16,
        (
            queries,
            below_keys,
            refreshed,
            above_keys,
            below_values,
            value_cache,
            above_values,
            stream,
        ),
        (segments.reshape(-1, row_count), mlp_gain),
        scalars=(position,),
        scratch=(pltpu.VMEM((row_count, model_width), jnp.float32),),
    )

    z_low = shift(normed, "z", 1)
    z_high = shift(normed, "z", -1)
    z_far = shift(normed, "z", 2)
    swapped = shift(normed, "c", 1)
    z_low_other = shift(z_low, "c", 1)
    z_high_other = shift(z_high, "c", 1)
    z_far_other = shift(z_far, "c", 1)
    mine, sent = pooled_parts(
        [normed, z_low, z_high, z_far],
        [swapped, z_low_other, z_high_other, z_far_other],
        weights,
        here,
        "mlp",
    )

    sums = mine + shift(sent, "c", 1).astype(jnp.float32)
    own = sums[:m]
    from_high = shift(sums[m : 2 * m].astype(jnp.bfloat16), "z", -1)
    from_low = shift(sums[2 * m : 3 * m].astype(jnp.bfloat16), "z", 1)
    from_far = shift(sums[3 * m :].astype(jnp.bfloat16), "z", 2)
    outgoing = call(
        merge_kernel,
        "merge",
        jax.ShapeDtypeStruct((tok_count * m, model_width), jnp.bfloat16),
        2 * m * model_width * model_width,
        16,
        (own, from_low, from_high, from_far, mixed_mean, w_merge),
        (b_proj, merge_gain, b_merge, owners),
        semaphores=9,
    ).reshape(tok_count, m, model_width)
    arrived = lax.all_to_all(outgoing, "tok", split_axis=0, concat_axis=0, tiled=True)
    delivered = arrived.reshape(1, 1, tok_count * m, model_width)
    return (refreshed, delivered)


def solution(mesh):
    fine = Mesh(mesh.devices.reshape(4, 4, 2, 4), ("x", "z", "c", "tok"))
    return jax.shard_map(
        body,
        mesh=fine,
        in_specs=(
            P(ROWS, None),
            P(ROWS, None),
            P(ROWS, None),
            P(ROWS, None),
            P("tok"),
            P(ROWS),
            P(ROWS),
            P(),
            P(),
            P(),
            P(),
            P(None, BLK),
            P(BLK),
            P(BLK, None),
            P(),
            P(),
            P(),
            P(),
        ),
        out_specs=(P(ROWS, None), P("tok", BLK, None, None)),
        check_vma=False,
    )
```
